32 devices in a mesh: gz: 8 (over z, core), xy: 4 (over y, x).
Axes of the slice: x: 2, y: 2, z: 4, core: 2. Of those that a mesh axis runs over, the one named last changes fastest.
Arguments:
- slab_image: float32 [32, 128, 1024], P('gz', None, 'xy'), may hold values from 0 to 1
- width_taps: float32 [16, 5], replicated, may hold values from -2.5 to 2.5
- height_taps: float32 [16, 5], replicated, may hold values from -2.5 to 2.5
- depth_taps: float32 [16, 5], replicated, may hold values from -2.5 to 2.5
- fragment_ids: int32 [32, 128, 1024], P(None, 'gz', 'xy'), may hold values from 0 to 1023, as said below
- fragment_owner: int32 [32768, 1], P(('gz', 'xy')), may hold values from 0 to 3, as said below
- coarse_centroids: float32 [16, 1024], P(None, ('gz', 'xy')), may hold values from -24 to 24
- parent_map: int32 [4096], P(('gz', 'xy')), may hold values from 0 to 31
- fine_offsets: float32 [16, 4096], P(None, ('gz', 'xy')), may hold values from -2.5 to 2.5
Outputs:
- fragment_means: float32 [16, 32768], P(None, ('gz', 'xy'))
- centroids: float32 [16, 4096], P(None, ('gz', 'xy'))
The draws below stay inside these ranges and needn't reach their ends.
Inputs may be any that keep to these rules, and one draw needn't show every extreme that they name: `fragment_ids`: ids are local to a pencil block of 32 x 16 x 256 voxels; every id 0 to 1023 occurs in every block. `fragment_owner`: of the 1024 fragments of one pencil block at most 512 name the same owner; in each row along xy some owner takes exactly 512 from every block of that row.
All inputs are finite; a program needn't handle non-finite values.
Results may differ from the reference program's by a relative error of at most 0.00038.
Values may be sent and summed in bfloat16 or wider, within the bound.
A program may use at most 128 MiB of HBM per device.

```python
import jax
import jax.numpy as jnp
from jax import lax

CH = 16
TAPS = 5
YCOL = 16
XROW = 256
BZ = 4
BY = 4
BX = 8
KF_DEV = 128
KC_DEV = 32
ITERS = 3
NZ = 32
NY = 128
NX = 1024
FL = 1024
NF = 32768
CAP = 512
KF = 4096
KC = 1024
PSEUDO = 1024
N_GZ = 8
N_XY = 4


def fragment_volume(key):
    devices = N_GZ * N_XY
    bricks_y = YCOL // BY
    bricks_x = XROW // BX
    zpos = jnp.arange(NZ, dtype=jnp.int32)[:, None, None]
    ypos = jnp.arange(YCOL, dtype=jnp.int32)[None, :, None]
    xpos = jnp.arange(XROW, dtype=jnp.int32)[None, None, :]
    brick = zpos // BZ * (bricks_y * bricks_x) + ypos // BY * bricks_x + xpos // BX
    moved = zpos // BZ * (bricks_y * bricks_x) + ypos // BY * bricks_x + (xpos // BX + 1) % bricks_x
    inner = zpos % BZ + ypos % BY + xpos % BX
    flag = jax.random.randint(jax.random.fold_in(key, 21), (devices, NZ, YCOL, XROW), 0, 8) == 0
    flag = jnp.logical_and(flag, (inner > 0)[None])
    brick = jnp.where(flag, moved[None], brick[None])
    keys = jax.random.split(jax.random.fold_in(key, 22), devices)
    relabel = jax.vmap(lambda single: jax.random.permutation(single, FL))(keys).astype(jnp.int32)
    local = jnp.take_along_axis(relabel, brick.reshape(devices, -1), axis=1)
    return local.reshape(devices, NZ, YCOL, XROW)


def arrange(local):
    grid = local.reshape(N_GZ, N_XY, NZ, YCOL, XROW)
    grid = jnp.transpose(grid, (2, 0, 3, 1, 4))
    return grid.reshape(NZ, NY, NX)


def draw_fragment_ids(key, part):
    return arrange(fragment_volume(key)).astype(jnp.int32)


def draw_slab_image(key, part):
    local = fragment_volume(key)
    devices = N_GZ * N_XY
    levels = jax.random.uniform(jax.random.fold_in(key, 23), (devices, FL), minval=-1.0, maxval=1.0)
    level = jnp.take_along_axis(levels, local.reshape(devices, -1), axis=1).reshape(local.shape)
    noise = jax.random.uniform(jax.random.fold_in(key, 24), local.shape, minval=-1.0, maxval=1.0)
    values = 0.5 + 0.3 * level + 0.2 * noise
    return arrange(values).astype(jnp.float32)


def draw_fragment_owner(key, part):
    devices = N_GZ * N_XY
    heavy = jax.random.randint(jax.random.fold_in(key, 41), (N_GZ, 1), 0, N_XY)
    heavy = jnp.repeat(heavy, N_XY, axis=0)
    rows = jnp.arange(FL, dtype=jnp.int32)[None, :]
    spill = min(FL - CAP, CAP // 2)
    others = N_XY - 1
    random_part = jax.random.randint(jax.random.fold_in(key, 42), (devices, FL), 0, others)
    offset_start = jax.random.randint(jax.random.fold_in(key, 43), (devices, 1), 0, others)
    cycled = (rows - CAP - spill + offset_start) % others
    offset = jnp.where(rows < CAP + spill, random_part, cycled)
    owner = jnp.where(rows < CAP, heavy, (heavy + 1 + offset) % N_XY)
    keys = jax.random.split(jax.random.fold_in(key, 44), devices)
    shuffle = jax.vmap(lambda single: jax.random.permutation(single, FL))(keys)
    owner = jnp.take_along_axis(owner, shuffle, axis=1)
    return owner.reshape(devices * FL, 1).astype(jnp.int32)


def draw_coarse_centroids(key, part):
    base = jnp.clip(jax.random.normal(jax.random.fold_in(key, 51), (CH, KC)), -4.0, 4.0) * 0.6
    return base.astype(jnp.float32)


def plant(drawn, key, smallest, top_value):
    place = [jax.random.randint(jax.random.fold_in(key, axis), (), 0, length) for axis, length in enumerate(drawn.shape)]
    longest = drawn.shape.index(max(drawn.shape))
    beside = place[:longest] + [(place[longest] + 1) % drawn.shape[longest]] + place[longest + 1:]
    return drawn.at[tuple(place)].set(smallest).at[tuple(beside)].set(top_value)


def level_of(stream_key, dims, pieces, low, largest):
    level = 1.0
    for axis_at, shards_of in pieces:
        heights = jax.random.uniform(jax.random.fold_in(jax.random.fold_in(stream_key, 6), axis_at), (shards_of,), jnp.float32, low / len(pieces), largest / len(pieces))
        level = level * jnp.repeat(jnp.exp(heights), dims[axis_at] // shards_of).reshape((-1,) + (1,) * (len(dims) - 1 - axis_at))
    return level


def scatter_about(key, dims, width, reach, cuts=(), kind=jnp.bfloat16):
    level = level_of(key, dims, cuts, -0.22, 0.18) if cuts else 1.0
    values = jax.random.normal(key, dims, jnp.float32) * width * level
    return jnp.minimum(jnp.maximum(values, -reach), reach).astype(kind)


def setup_inputs(seed: int = 0) -> dict:
    key_of = jax.random.split(jax.random.key(seed), 10)
    return {
        "slab_image": draw_slab_image(jax.random.fold_in(key_of[9], 71), 0),
        "width_taps": scatter_about(key_of[1], (CH, TAPS), 0.5, 2.5, (), jnp.float32),
        "height_taps": scatter_about(key_of[2], (CH, TAPS), 0.5, 2.5, (), jnp.float32),
        "depth_taps": scatter_about(key_of[3], (CH, TAPS), 0.5, 2.5, (), jnp.float32),
        "fragment_ids": draw_fragment_ids(jax.random.fold_in(key_of[9], 71), 0),
        "fragment_owner": draw_fragment_owner(jax.random.fold_in(key_of[9], 71), 0),
        "coarse_centroids": draw_coarse_centroids(jax.random.fold_in(key_of[9], 71), 0),
        "parent_map": plant(jax.random.randint(key_of[7], (KF,), 0, KC_DEV), jax.random.fold_in(key_of[7], 1), 0, KC_DEV - 1).astype(jnp.int32),
        "fine_offsets": scatter_about(key_of[8], (CH, KF), 0.25, 2.5, ((1, 32),), jnp.float32),
    }


HIGH = lax.Precision.HIGHEST
sharpness = 2.0


def planar_channel(volume, width_tap, height_tap):
    half = TAPS // 2
    padded = jnp.pad(volume, ((0, 0), (half, half), (half, half)))
    rows = volume.shape[1]
    cols = volume.shape[2]
    across = width_tap[0] * padded[:, :, 0:cols]
    for tap_shift in range(1, TAPS):
        across = across + width_tap[tap_shift] * padded[:, :, tap_shift:tap_shift + cols]
    planar = height_tap[0] * across[:, 0:rows, :]
    for tap_shift in range(1, TAPS):
        planar = planar + height_tap[tap_shift] * across[:, tap_shift:tap_shift + rows, :]
    return planar.astype(jnp.bfloat16)


def soft_stats(frags, weight, cents, allowed):
    cross = lax.dot_general(frags, cents, (((0,), (0,)), ((), ())), precision=HIGH, preferred_element_type=jnp.float32)
    distance = jnp.sum(frags * frags, axis=0)[:, None] + jnp.sum(cents * cents, axis=0)[None, :] - 2.0 * cross
    scores = jnp.where(allowed, -sharpness * distance, -jnp.inf)
    top = jnp.max(scores, axis=1, keepdims=True)
    expo = jnp.exp(scores - top)
    resp = expo / jnp.sum(expo, axis=1, keepdims=True)
    numer = jnp.dot(frags * weight[None, :], resp, precision=HIGH, preferred_element_type=jnp.float32)
    denom = jnp.dot(weight[None, :], resp, precision=HIGH, preferred_element_type=jnp.float32)
    return numer, denom[0]


def reference(slab_image, width_taps, height_taps, depth_taps, fragment_ids, fragment_owner, coarse_centroids, parent_map, fine_offsets):
    half = TAPS // 2
    ypos = jnp.arange(NY, dtype=jnp.int32)[None, :, None] // YCOL
    xpos = jnp.arange(NX, dtype=jnp.int32)[None, None, :] // XROW
    labels = ((ypos * N_XY + xpos) * FL + fragment_ids).astype(jnp.int32)
    flat_labels = labels.reshape(-1)

    def channel_terms(taps):
        width_tap, height_tap, depth_tap = taps
        planar = planar_channel(slab_image, width_tap, height_tap)
        planar = lax.optimization_barrier(planar).astype(jnp.float32)
        padded = jnp.pad(planar, ((half, half), (0, 0), (0, 0)))
        response = depth_tap[0] * padded[0:NZ]
        for tap_shift in range(1, TAPS):
            response = response + depth_tap[tap_shift] * padded[tap_shift:tap_shift + NZ]
        feature = jnp.tanh(response).astype(jnp.bfloat16)
        feature = lax.optimization_barrier(feature).astype(jnp.float32)
        return jax.ops.segment_sum(feature.reshape(-1), flat_labels, num_segments=NF)

    feature_sum = lax.map(channel_terms, (width_taps, height_taps, depth_taps))
    voxel_count = jax.ops.segment_sum(jnp.ones(flat_labels.shape, jnp.float32), flat_labels, num_segments=NF)
    fragment_means = feature_sum / voxel_count[None, :]

    block = jnp.arange(KF, dtype=jnp.int32) // KF_DEV
    columns = (block * KC_DEV + parent_map).astype(jnp.int32)
    centroids = coarse_centroids[:, columns] + fine_offsets
    owner = fragment_owner[:, 0]
    span = N_XY * KF_DEV
    column_owner = jnp.arange(span, dtype=jnp.int32) // KF_DEV
    pseudo = float(PSEUDO)

    for step in range(ITERS):
        def visit(carry, device):
            numer, denom = carry
            row_start = ((device // N_XY) * span).astype(jnp.int32)
            frag_start = (device * FL).astype(jnp.int32)
            frags = lax.dynamic_slice_in_dim(fragment_means, frag_start, FL, 1)
            weight = lax.dynamic_slice_in_dim(voxel_count, frag_start, FL, 0)
            own = lax.dynamic_slice_in_dim(owner, frag_start, FL, 0)
            cents = lax.dynamic_slice_in_dim(centroids, row_start, span, 1)
            part_num, part_den = soft_stats(frags, weight, cents, own[:, None] == column_owner[None, :])
            numer = lax.dynamic_update_slice_in_dim(numer, lax.dynamic_slice_in_dim(numer, row_start, span, 1) + part_num, row_start, 1)
            denom = lax.dynamic_update_slice_in_dim(denom, lax.dynamic_slice_in_dim(denom, row_start, span, 0) + part_den, row_start, 0)
            return (numer, denom), None

        start_carry = (jnp.zeros((CH, KF), jnp.float32), jnp.zeros((KF,), jnp.float32))
        carried = lax.scan(visit, start_carry, jnp.arange(N_GZ * N_XY, dtype=jnp.int32))[0]
        centroids = (carried[0] + pseudo * centroids) / (carried[1][None, :] + pseudo)
    return fragment_means, centroids
```

```python
import functools

import jax
import jax.numpy as jnp
from jax import lax
from jax.experimental import pallas as pl
from jax.experimental.pallas import tpu as pltpu
from jax.sharding import PartitionSpec as P

TAPS = 5
HALF = TAPS // 2
ITERS = 3
HIGH = lax.Precision.HIGHEST
sharpness = 2.0
LO = 128
ROWS = 4
F32 = jnp.float32
BF16 = jnp.bfloat16


def with_halo(cells, axis, dim, width):
    count = lax.axis_size(axis)
    ends = count - 1
    head = lax.slice_in_dim(cells, 0, width, axis=dim)
    tail = lax.slice_in_dim(cells, cells.shape[dim] - width, cells.shape[dim], axis=dim)
    return jnp.concatenate(
        [
            lax.ppermute(tail, axis, [(i, i + 1) for i in range(ends)]),
            cells,
            lax.ppermute(head, axis, [(i + 1, i) for i in range(ends)]),
        ],
        axis=dim,
    )


def feature_kernel(img, ids, taps, owner, pay_ref, means_ref, shift, across, planar, acc):
    depth, rows, cols = ids.shape
    padded_rows = rows + TAPS - 1
    fragments = means_ref.shape[1]
    highs = fragments // LO
    chans = means_ref.shape[0]
    lanes = pay_ref.shape[0] - chans
    for b in range(TAPS):
        shift[b] = img[:, b : b + cols]
    for e in range(HALF):
        planar[e] = jnp.zeros(planar.shape[1:], F32)
        planar[depth + HALF + e] = jnp.zeros(planar.shape[1:], F32)
    acc[...] = jnp.zeros(acc.shape, F32)

    def tap(kind, at):
        return jnp.broadcast_to(taps[:, kind * TAPS + at : kind * TAPS + at + 1], (chans, cols))

    def plane(z, carry):
        for y in range(padded_rows):
            total = None
            for b in range(TAPS):
                row = shift[b, pl.ds(z * padded_rows + y, 1), :]
                term = tap(0, b) * jnp.broadcast_to(row, (chans, cols))
                total = term if total is None else total + term
            across[y] = total
        for y in range(rows):
            total = tap(1, 0) * across[y]
            for a in range(1, TAPS):
                total = total + tap(1, a) * across[y + a]
            planar[z + HALF, y] = total.astype(BF16).astype(F32)
        return carry

    lax.fori_loop(0, depth, plane, 0)
    low_line = lax.broadcasted_iota(jnp.int32, (LO, cols), 0).astype(F32).astype(BF16)
    high_line = lax.broadcasted_iota(jnp.int32, (16, cols), 0).astype(F32).astype(BF16)
    one = jnp.ones((16, cols), BF16)
    zero = jnp.zeros((16, cols), BF16)

    def gather_sums(step, carry):
        z = step // (rows // ROWS)
        base = (step % (rows // ROWS)) * ROWS
        left, right = [], []
        for r in range(ROWS):
            y = base + r
            total = tap(2, 0) * planar[z, y]
            for e in range(1, TAPS):
                total = total + tap(2, e) * planar[z + e, y]
            feat = jnp.tanh(total).astype(BF16)
            idrow = ids[z, pl.ds(y, 1), :]
            high = jnp.broadcast_to((idrow // LO).astype(F32), (16, cols)).astype(BF16)
            low = jnp.broadcast_to((idrow % LO).astype(F32), (16, cols)).astype(BF16)
            parts = [
                jnp.where(high == jnp.full((16, cols), h, BF16), feat, zero) for h in range(highs)
            ]
            parts.append(jnp.where(high == high_line, one, zero))
            left.append(jnp.concatenate(parts, axis=0))
            right.append(
                jnp.concatenate(
                    [
                        jnp.where(low == low_line[k * 16 : (k + 1) * 16], one, zero)
                        for k in range(LO // 16)
                    ],
                    axis=0,
                )
            )
        acc[...] += lax.dot_general(
            jnp.concatenate(left, axis=1),
            jnp.concatenate(right, axis=1),
            (((1,), (1,)), ((), ())),
            preferred_element_type=F32,
        )
        return carry

    lax.fori_loop(0, depth * (rows // ROWS), gather_sums, 0)
    for h in range(highs):
        count = acc[highs * chans + h : highs * chans + h + 1, :]
        mean = acc[h * chans : (h + 1) * chans, :] / count
        means_ref[:, h * LO : (h + 1) * LO] = mean
        pay_ref[:chans, h * LO : (h + 1) * LO] = mean
        own = jnp.broadcast_to(owner[:, h * LO : (h + 1) * LO], (lanes, LO))
        line = lax.broadcasted_iota(jnp.int32, (lanes, LO), 0)
        pay_ref[chans:, h * LO : (h + 1) * LO] = jnp.where(
            own == line, jnp.broadcast_to(count, (lanes, LO)), 0.0
        )


def split3(x):
    high = x.astype(BF16)
    rest = x - high.astype(F32)
    mid = rest.astype(BF16)
    low = (rest - mid.astype(F32)).astype(BF16)
    return high, mid, low


def refine_kernel(pseudo, pay, weight, coarse, parent, offsets, out_ref, factors, norms):
    sources, chans, fragments = pay.shape
    coarse_count = coarse.shape[1]
    fine = out_ref.shape[1]
    select = (
        jnp.broadcast_to(parent[...], (coarse_count, fine))
        == lax.broadcasted_iota(jnp.int32, (coarse_count, fine), 0)
    ).astype(F32)
    cents = jnp.dot(coarse[...], select, precision=HIGH, preferred_element_type=F32) + offsets[...]

    def prepare(s, carry):
        frags = pay[s]
        fh, fm, fl = split3(-2.0 * frags)
        ones = jnp.ones((3 * chans, fragments), BF16)
        factors[s] = jnp.concatenate([fh, fm, fh, fl, fm, fh, ones], axis=0)
        norms[s] = jnp.sum(frags * frags, axis=0, keepdims=True)
        return carry

    lax.fori_loop(0, sources, prepare, 0)
    for step in range(ITERS):
        ch, cm, cl = split3(cents)
        sh, sm, sl = split3(cents * cents)
        keys = jnp.concatenate([ch, ch, cm, ch, cm, cl, sh, sm, sl], axis=0)

        def visit(s, total):
            distance = norms[s] + lax.dot_general(
                keys, factors[s], (((0,), (0,)), ((), ())), preferred_element_type=F32
            )
            scores = -sharpness * distance
            top = jnp.max(scores, axis=0, keepdims=True)
            expo = jnp.exp(scores - top)
            scale = weight[s] / jnp.sum(expo, axis=0, keepdims=True)
            scale = jnp.broadcast_to(scale, (chans, fragments))
            gh, gm, gl = split3(jnp.concatenate([pay[s] * scale, scale], axis=0))
            eh, em, el = split3(expo)
            dims = (((1,), (1,)), ((), ()))
            first = lax.dot_general(
                jnp.concatenate([gh, gm, gl], axis=0), eh, dims, preferred_element_type=F32
            )
            second = lax.dot_general(
                jnp.concatenate([gh, gm], axis=0), em, dims, preferred_element_type=F32
            )
            size = 2 * chans
            return (
                total
                + (first[2 * size :] + second[size:])
                + (first[size : 2 * size] + second[:size])
                + first[:size]
            )

        total = lax.fori_loop(0, sources, visit, jnp.zeros((2 * chans, fine), F32))
        cents = (total[:chans] + pseudo * cents) / (total[chans:] + pseudo)
    out_ref[...] = cents


def shards(
    slab_image,
    width_taps,
    height_taps,
    depth_taps,
    fragment_ids,
    fragment_owner,
    coarse_centroids,
    parent_map,
    fine_offsets,
):
    chans = width_taps.shape[0]
    depth, rows, cols = fragment_ids.shape
    fragments = fragment_owner.shape[0]
    lanes = lax.axis_size("xy")
    stacks = lax.axis_size("gz")
    padded_rows = rows + TAPS - 1
    rimmed = with_halo(slab_image, "xy", 2, HALF)
    rimmed = jnp.pad(rimmed, ((0, 0), (HALF, HALF), (0, 0)))
    blocks = jnp.stack([rimmed[:, j * rows : j * rows + padded_rows] for j in range(stacks)])
    pencil = lax.all_to_all(blocks, "gz", split_axis=0, concat_axis=0, tiled=True)
    pencil = pencil.reshape(depth * padded_rows, cols + TAPS - 1)
    taps = jnp.concatenate([width_taps, height_taps, depth_taps], axis=1)
    highs = fragments // LO
    assert highs <= 16
    pay, means = pl.pallas_call(
        feature_kernel,
        out_shape=(
            jax.ShapeDtypeStruct((chans + lanes, fragments), F32),
            jax.ShapeDtypeStruct((chans, fragments), F32),
        ),
        in_specs=[pl.BlockSpec(memory_space=pltpu.VMEM)] * 4,
        out_specs=(pl.BlockSpec(memory_space=pltpu.VMEM),) * 2,
        scratch_shapes=[
            pltpu.VMEM((TAPS, depth * padded_rows, cols), F32),
            pltpu.VMEM((padded_rows, chans, cols), F32),
            pltpu.VMEM((depth + 2 * HALF, rows, chans, cols), F32),
            pltpu.VMEM((highs * chans + 16, LO), F32),
        ],
        compiler_params=pltpu.CompilerParams(vmem_limit_bytes=56 << 20),
        name="features",
    )(pencil, fragment_ids, taps, fragment_owner.reshape(1, fragments))
    gathered = lax.all_gather(pay, "xy", axis=0)
    me = lax.axis_index("xy")
    weight = lax.dynamic_slice_in_dim(gathered, chans + me, 1, axis=1)
    fine = fine_offsets.shape[1]
    pseudo = float(fragment_ids.size // fine)
    centroids = pl.pallas_call(
        functools.partial(refine_kernel, pseudo),
        out_shape=jax.ShapeDtypeStruct((chans, fine), F32),
        in_specs=[pl.BlockSpec(memory_space=pltpu.VMEM)] * 5,
        out_specs=pl.BlockSpec(memory_space=pltpu.VMEM),
        scratch_shapes=[
            pltpu.VMEM((lanes, 9 * chans, fragments), BF16),
            pltpu.VMEM((lanes, 1, fragments), F32),
        ],
        compiler_params=pltpu.CompilerParams(vmem_limit_bytes=48 << 20),
        name="refine",
    )(gathered[:, :chans], weight, coarse_centroids, parent_map.reshape(1, fine), fine_offsets)
    return (means, centroids)


def solution(mesh):
    placed = (
        P("gz", None, "xy"),
        P(),
        P(),
        P(),
        P(None, "gz", "xy"),
        P(("gz", "xy"), None),
        P(None, ("gz", "xy")),
        P(("gz", "xy")),
        P(None, ("gz", "xy")),
    )
    return jax.shard_map(
        shards,
        mesh=mesh,
        in_specs=placed,
        out_specs=(P(None, ("gz", "xy")), P(None, ("gz", "xy"))),
        check_vma=False,
    )
```

```python
import functools

import jax
import jax.numpy as jnp
from jax import lax
from jax.experimental import pallas as pl
from jax.experimental.pallas import tpu as pltpu
from jax.sharding import PartitionSpec as P

TAPS = 5
HALF = TAPS // 2
ITERS = 3
HIGH = lax.Precision.HIGHEST
sharpness = 2.0
LO = 128
ROWS = 4
F32 = jnp.float32
BF16 = jnp.bfloat16


MESH = pl.DeviceIdType.MESH
LANE = 128


def exchange_kernel(rows, img, out, blocks, edges, halo, turned, send, recv, side_send, side_recv):
    here = lax.axis_index("gz")
    lane = lax.axis_index("xy")
    stacks = lax.axis_size("gz")
    lanes = lax.axis_size("xy")
    depth, height, cols = img.shape
    padded = rows + TAPS - 1
    size = depth * padded
    wide = depth * HALF

    for side in range(2):
        if stacks * wide < LANE:
            halo[side, stacks * wide :, :] = jnp.zeros((LANE - stacks * wide, height), F32)

    @pl.when(lane == 0)
    def _():
        halo[0] = jnp.zeros(halo.shape[1:], F32)

    @pl.when(lane == lanes - 1)
    def _():
        halo[1] = jnp.zeros(halo.shape[1:], F32)

    barrier = pltpu.get_barrier_semaphore()

    def greet(d, carry):
        j = lax.rem(here + d, stacks)

        @pl.when(d > 0)
        def _():
            pl.semaphore_signal(barrier, inc=1, device_id=(j, lane), device_id_type=MESH)

        @pl.when(lane > 0)
        def _():
            pl.semaphore_signal(barrier, inc=1, device_id=(j, lane - 1), device_id_type=MESH)

        @pl.when(lane < lanes - 1)
        def _():
            pl.semaphore_signal(barrier, inc=1, device_id=(j, lane + 1), device_id_type=MESH)

        return carry

    lax.fori_loop(0, stacks, greet, 0)
    for j in range(stacks):
        for z in range(depth):
            start = j * rows - HALF
            low, high = max(start, 0), min(start + padded, height)
            at = z * padded
            if low > start:
                blocks[j, at : at + low - start, :] = jnp.zeros((low - start, cols), F32)
            if high < start + padded:
                blocks[j, at + high - start : at + padded, :] = jnp.zeros(
                    (start + padded - high, cols), F32
                )
            blocks[j, at + low - start : at + high - start, :] = img[z, low:high, :]
    for z in range(depth):
        first = jnp.transpose(img[z, :, :LANE])
        last = jnp.transpose(img[z, :, cols - LANE :])
        edges[0, z * HALF : (z + 1) * HALF, :] = last[LANE - HALF :, :]
        edges[1, z * HALF : (z + 1) * HALF, :] = first[:HALF, :]
    sides = lax.div(lane + lanes - 1, lanes) + lax.div(2 * lanes - 2 - lane, lanes)
    pl.semaphore_wait(barrier, stacks - 1 + stacks * sides)

    def main_copy(j, source):
        return pltpu.make_async_remote_copy(
            src_ref=blocks.at[j],
            dst_ref=out.at[pl.ds(pl.multiple_of(source * size, 8), size), LANE : LANE + cols],
            send_sem=send.at[j],
            recv_sem=recv.at[source],
            device_id=(j, lane),
            device_id_type=MESH,
        )

    def side_copy(side, j, source, target):
        return pltpu.make_async_remote_copy(
            src_ref=edges.at[side],
            dst_ref=halo.at[side, pl.ds(pl.multiple_of(source * wide, 8), wide), :],
            send_sem=side_send.at[side, j],
            recv_sem=side_recv.at[side, source],
            device_id=(j, target),
            device_id_type=MESH,
        )

    def start(d, carry):
        j = lax.rem(here + d, stacks)

        @pl.when(d > 0)
        def _():
            main_copy(j, here).start()

        @pl.when(lane < lanes - 1)
        def _():
            side_copy(0, j, here, lane + 1).start()

        @pl.when(lane > 0)
        def _():
            side_copy(1, j, here, lane - 1).start()

        return carry

    lax.fori_loop(0, stacks, start, 0)
    out[pl.ds(pl.multiple_of(here * size, 8), size), LANE : LANE + cols] = blocks[here]

    def finish(d, carry):
        j = lax.rem(here + d, stacks)

        @pl.when(d > 0)
        def _():
            main_copy(j, here).wait_send()
            main_copy(j, j).wait_recv()

        @pl.when(lane < lanes - 1)
        def _():
            side_copy(0, j, here, lane + 1).wait_send()
            side_copy(1, j, j, lane + 1).wait_recv()

        @pl.when(lane > 0)
        def _():
            side_copy(1, j, here, lane - 1).wait_send()
            side_copy(0, j, j, lane - 1).wait_recv()

        return carry

    lax.fori_loop(0, stacks, finish, 0)
    for side in range(2):
        turned[:8, :] = jnp.zeros((8, LANE), F32)
        turned[8 + height :, :] = jnp.zeros((8, LANE), F32)
        turned[8 : 8 + height, :] = jnp.transpose(halo[side])
        strip = turned[pl.ds(here * rows + 8 - HALF, padded), :]
        for z in range(stacks * depth):
            place = LANE - HALF if side == 0 else LANE + cols
            out[z * padded : (z + 1) * padded, place : place + HALF] = strip[
                :, z * HALF : (z + 1) * HALF
            ]


def gather_kernel(pay, out, send, recv):
    here = lax.axis_index("gz")
    lane = lax.axis_index("xy")
    lanes = lax.axis_size("xy")
    barrier = pltpu.get_barrier_semaphore()
    for d in range(1, lanes):
        pl.semaphore_signal(
            barrier, inc=1, device_id=(here, lax.rem(lane + d, lanes)), device_id_type=MESH
        )
    pl.semaphore_wait(barrier, lanes - 1)

    def copy(target, source):
        return pltpu.make_async_remote_copy(
            src_ref=pay,
            dst_ref=out.at[source],
            send_sem=send.at[target],
            recv_sem=recv.at[source],
            device_id=(here, target),
            device_id_type=MESH,
        )

    for d in range(1, lanes):
        copy(lax.rem(lane + d, lanes), lane).start()
    out[lane] = pay[...]
    for d in range(1, lanes):
        other = lax.rem(lane + d, lanes)
        copy(other, lane).wait_send()
        copy(other, other).wait_recv()


def feature_kernel(img, ids, taps, owner, pay_ref, means_ref, shift, planar, highs_f, lows_f, acc):
    depth, rows, cols = ids.shape
    padded_rows = rows + TAPS - 1
    fragments = means_ref.shape[1]
    highs = fragments // LO
    chans = means_ref.shape[0]
    lanes = pay_ref.shape[0] - chans
    for b in range(TAPS):
        for x in range(0, cols, LANE):
            start = LANE - HALF + b + x
            shift[b, x // LANE] = img[:, start : start + LANE]
    for e in range(HALF):
        planar[e] = jnp.zeros(planar.shape[1:], F32)
        planar[depth + HALF + e] = jnp.zeros(planar.shape[1:], F32)
    acc[...] = jnp.zeros(acc.shape, F32)

    def divide(z, carry):
        for x in range(0, cols, LANE):
            part = ids[z, :, x : x + LANE]
            highs_f[x // LANE, z] = (part >> (LO.bit_length() - 1)).astype(F32)
            lows_f[x // LANE, z] = (part & (LO - 1)).astype(F32)
        return carry

    lax.fori_loop(0, depth, divide, 0)
    tap = [jnp.broadcast_to(taps[:, i : i + 1], (chans, LANE)) for i in range(3 * TAPS)]

    def plane(z, carry):
        for x in range(0, cols, LANE):
            window = []
            for y in range(padded_rows):
                total = None
                for b in range(TAPS):
                    row = shift[b, x // LANE, pl.ds(z * padded_rows + y, 1), :]
                    term = tap[b] * jnp.broadcast_to(row, (chans, LANE))
                    total = term if total is None else total + term
                window.append(total)
                if y >= TAPS - 1:
                    total = tap[TAPS] * window[y - TAPS + 1]
                    for a in range(1, TAPS):
                        total = total + tap[TAPS + a] * window[y - TAPS + 1 + a]
                    planar[z + HALF, y - TAPS + 1, :, x : x + LANE] = total.astype(BF16).astype(F32)
        return carry

    lax.fori_loop(0, depth, plane, 0)
    low_line = lax.broadcasted_iota(jnp.int32, (LO, LANE), 0).astype(F32).astype(BF16)
    one = jnp.ones((16, LANE), BF16)
    zero = jnp.zeros((16, LANE), BF16)

    def gather_sums(step, carry):
        z = step // (rows // ROWS)
        base = (step % (rows // ROWS)) * ROWS
        left, right = [], []
        for r in range(ROWS):
            y = base + r
            for x in range(0, cols, LANE):
                total = tap[2 * TAPS] * planar[z, y, :, x : x + LANE]
                for e in range(1, TAPS):
                    total = total + tap[2 * TAPS + e] * planar[z + e, y, :, x : x + LANE]
                feat = jnp.tanh(total).astype(BF16)
                high = highs_f[x // LANE, z, pl.ds(y, 1), :]
                high = jnp.broadcast_to(high, (16, LANE)).astype(BF16)
                low = lows_f[x // LANE, z, pl.ds(y, 1), :]
                low = jnp.broadcast_to(low, (16, LANE)).astype(BF16)
                parts = [
                    jnp.where(high == jnp.full((16, LANE), h, BF16), feat, zero)
                    for h in range(highs)
                ]
                parts.append(jnp.where(high == low_line[:16], one, zero))
                left.append(jnp.concatenate(parts, axis=0))
                right.append(
                    jnp.concatenate(
                        [
                            jnp.where(low == low_line[k * 16 : (k + 1) * 16], one, zero)
                            for k in range(LO // 16)
                        ],
                        axis=0,
                    )
                )
        acc[...] += lax.dot_general(
            jnp.concatenate(left, axis=1),
            jnp.concatenate(right, axis=1),
            (((1,), (1,)), ((), ())),
            preferred_element_type=F32,
        )
        return carry

    lax.fori_loop(0, depth * (rows // ROWS), gather_sums, 0)
    for h in range(highs):
        count = acc[highs * chans + h : highs * chans + h + 1, :]
        mean = acc[h * chans : (h + 1) * chans, :] / count
        means_ref[:, h * LO : (h + 1) * LO] = mean
        pay_ref[:chans, h * LO : (h + 1) * LO] = mean
        own = jnp.broadcast_to(owner[:, h * LO : (h + 1) * LO], (lanes, LO))
        line = lax.broadcasted_iota(jnp.int32, (lanes, LO), 0)
        pay_ref[chans:, h * LO : (h + 1) * LO] = jnp.where(
            own == line, jnp.broadcast_to(count, (lanes, LO)), 0.0
        )


def split3(x):
    high = x.astype(BF16)
    rest = x - high.astype(F32)
    mid = rest.astype(BF16)
    low = (rest - mid.astype(F32)).astype(BF16)
    return high, mid, low


def refine_kernel(pseudo, pay, coarse, parent, offsets, out_ref, factors, norms):
    sources, _, fragments = pay.shape
    chans = out_ref.shape[0]
    own = chans + lax.axis_index("xy")
    coarse_count = coarse.shape[1]
    fine = out_ref.shape[1]
    select = (
        jnp.broadcast_to(parent[...], (coarse_count, fine))
        == lax.broadcasted_iota(jnp.int32, (coarse_count, fine), 0)
    ).astype(F32)
    cents = jnp.dot(coarse[...], select, precision=HIGH, preferred_element_type=F32) + offsets[...]

    def prepare(s, carry):
        frags = pay[s, :chans, :]
        fh, fm, fl = split3(-2.0 * frags)
        ones = jnp.ones((3 * chans, fragments), BF16)
        factors[s] = jnp.concatenate([fh, fm, fh, fl, fm, fh, ones], axis=0)
        norms[s] = jnp.sum(frags * frags, axis=0, keepdims=True)
        return carry

    lax.fori_loop(0, sources, prepare, 0)
    for step in range(ITERS):
        ch, cm, cl = split3(cents)
        sh, sm, sl = split3(cents * cents)
        keys = jnp.concatenate([ch, ch, cm, ch, cm, cl, sh, sm, sl], axis=0)

        def visit(s, total):
            distance = norms[s] + lax.dot_general(
                keys, factors[s], (((0,), (0,)), ((), ())), preferred_element_type=F32
            )
            scores = -sharpness * distance
            top = jnp.max(scores, axis=0, keepdims=True)
            expo = jnp.exp(scores - top)
            scale = pay[s, pl.ds(own, 1), :] / jnp.sum(expo, axis=0, keepdims=True)
            scale = jnp.broadcast_to(scale, (chans, fragments))
            gh, gm, gl = split3(jnp.concatenate([pay[s, :chans, :] * scale, scale], axis=0))
            eh, em, el = split3(expo)
            dims = (((1,), (1,)), ((), ()))
            first = lax.dot_general(
                jnp.concatenate([gh, gm, gl], axis=0), eh, dims, preferred_element_type=F32
            )
            second = lax.dot_general(
                jnp.concatenate([gh, gm], axis=0), em, dims, preferred_element_type=F32
            )
            size = 2 * chans
            return (
                total
                + (first[2 * size :] + second[size:])
                + (first[size : 2 * size] + second[:size])
                + first[:size]
            )

        total = lax.fori_loop(0, sources, visit, jnp.zeros((2 * chans, fine), F32))
        cents = (total[:chans] + pseudo * cents) / (total[chans:] + pseudo)
    out_ref[...] = cents


def shards(
    slab_image,
    width_taps,
    height_taps,
    depth_taps,
    fragment_ids,
    fragment_owner,
    coarse_centroids,
    parent_map,
    fine_offsets,
):
    chans = width_taps.shape[0]
    depth, rows, cols = fragment_ids.shape
    fragments = fragment_owner.shape[0]
    lanes = lax.axis_size("xy")
    stacks = lax.axis_size("gz")
    padded_rows = rows + TAPS - 1
    slab_depth, height, _ = slab_image.shape
    pencil = pl.pallas_call(
        functools.partial(exchange_kernel, rows),
        out_shape=jax.ShapeDtypeStruct((depth * padded_rows, cols + 2 * LANE), F32),
        in_specs=[pl.BlockSpec(memory_space=pltpu.VMEM)],
        out_specs=pl.BlockSpec(memory_space=pltpu.VMEM),
        scratch_shapes=[
            pltpu.VMEM((stacks, slab_depth * padded_rows, cols), F32),
            pltpu.VMEM((2, slab_depth * HALF, height), F32),
            pltpu.VMEM((2, LANE, height), F32),
            pltpu.VMEM((height + 16, LANE), F32),
            pltpu.SemaphoreType.DMA((stacks,)),
            pltpu.SemaphoreType.DMA((stacks,)),
            pltpu.SemaphoreType.DMA((2, stacks)),
            pltpu.SemaphoreType.DMA((2, stacks)),
        ],
        compiler_params=pltpu.CompilerParams(
            collective_id=0, has_side_effects=True, vmem_limit_bytes=32 << 20
        ),
        name="exchange",
    )(slab_image)
    taps = jnp.concatenate([width_taps, height_taps, depth_taps], axis=1)
    highs = fragments // LO
    assert highs <= 16
    pay, means = pl.pallas_call(
        feature_kernel,
        out_shape=(
            jax.ShapeDtypeStruct((chans + lanes, fragments), F32),
            jax.ShapeDtypeStruct((chans, fragments), F32),
        ),
        in_specs=[pl.BlockSpec(memory_space=pltpu.VMEM)] * 4,
        out_specs=(pl.BlockSpec(memory_space=pltpu.VMEM),) * 2,
        scratch_shapes=[
            pltpu.VMEM((TAPS, cols // LANE, depth * padded_rows, LANE), F32),
            pltpu.VMEM((depth + 2 * HALF, rows, chans, cols), F32),
            pltpu.VMEM((cols // LANE, depth, rows, LANE), F32),
            pltpu.VMEM((cols // LANE, depth, rows, LANE), F32),
            pltpu.VMEM((highs * chans + 16, LO), F32),
        ],
        compiler_params=pltpu.CompilerParams(vmem_limit_bytes=56 << 20),
        name="features",
    )(pencil, fragment_ids, taps, fragment_owner.reshape(1, fragments))
    gathered = pl.pallas_call(
        gather_kernel,
        out_shape=jax.ShapeDtypeStruct((lanes,) + pay.shape, F32),
        in_specs=[pl.BlockSpec(memory_space=pltpu.VMEM)],
        out_specs=pl.BlockSpec(memory_space=pltpu.VMEM),
        scratch_shapes=[pltpu.SemaphoreType.DMA((lanes,)), pltpu.SemaphoreType.DMA((lanes,))],
        compiler_params=pltpu.CompilerParams(
            collective_id=1, has_side_effects=True, vmem_limit_bytes=32 << 20
        ),
        name="gather",
    )(pay)
    fine = fine_offsets.shape[1]
    pseudo = float(fragment_ids.size // fine)
    centroids = pl.pallas_call(
        functools.partial(refine_kernel, pseudo),
        out_shape=jax.ShapeDtypeStruct((chans, fine), F32),
        in_specs=[pl.BlockSpec(memory_space=pltpu.VMEM)] * 4,
        out_specs=pl.BlockSpec(memory_space=pltpu.VMEM),
        scratch_shapes=[
            pltpu.VMEM((lanes, 9 * chans, fragments), BF16),
            pltpu.VMEM((lanes, 1, fragments), F32),
        ],
        compiler_params=pltpu.CompilerParams(vmem_limit_bytes=48 << 20),
        name="refine",
    )(gathered, coarse_centroids, parent_map.reshape(1, fine), fine_offsets)
    return (means, centroids)


def solution(mesh):
    placed = (
        P("gz", None, "xy"),
        P(),
        P(),
        P(),
        P(None, "gz", "xy"),
        P(("gz", "xy"), None),
        P(None, ("gz", "xy")),
        P(("gz", "xy")),
        P(None, ("gz", "xy")),
    )
    return jax.shard_map(
        shards,
        mesh=mesh,
        in_specs=placed,
        out_specs=(P(None, ("gz", "xy")), P(None, ("gz", "xy"))),
        check_vma=False,
    )
```

```python
import functools

import jax
import jax.numpy as jnp
from jax import lax
from jax.experimental import pallas as pl
from jax.experimental.pallas import tpu as pltpu
from jax.sharding import PartitionSpec as P

TAPS = 5
HALF = TAPS // 2
ITERS = 3
HIGH = lax.Precision.HIGHEST
sharpness = 2.0
LO = 128
ROWS = 16
F32 = jnp.float32
BF16 = jnp.bfloat16


MESH = pl.DeviceIdType.MESH
LANE = 128


def exchange_kernel(rows, img, out, blocks, edges, halo, turned, send, recv, side_send, side_recv):
    here = lax.axis_index("gz")
    lane = lax.axis_index("xy")
    stacks = lax.axis_size("gz")
    lanes = lax.axis_size("xy")
    depth, height, cols = img.shape
    padded = rows + TAPS - 1
    size = depth * padded
    wide = depth * HALF

    for side in range(2):
        if stacks * wide < LANE:
            halo[side, stacks * wide :, :] = jnp.zeros((LANE - stacks * wide, height), F32)

    @pl.when(lane == 0)
    def _():
        halo[0] = jnp.zeros(halo.shape[1:], F32)

    @pl.when(lane == lanes - 1)
    def _():
        halo[1] = jnp.zeros(halo.shape[1:], F32)

    barrier = pltpu.get_barrier_semaphore()

    def greet(d, carry):
        j = lax.rem(here + d, stacks)

        @pl.when(d > 0)
        def _():
            pl.semaphore_signal(barrier, inc=1, device_id=(j, lane), device_id_type=MESH)

        @pl.when(lane > 0)
        def _():
            pl.semaphore_signal(barrier, inc=1, device_id=(j, lane - 1), device_id_type=MESH)

        @pl.when(lane < lanes - 1)
        def _():
            pl.semaphore_signal(barrier, inc=1, device_id=(j, lane + 1), device_id_type=MESH)

        return carry

    lax.fori_loop(0, stacks, greet, 0)
    for j in range(stacks):
        for z in range(depth):
            start = j * rows - HALF
            low, high = max(start, 0), min(start + padded, height)
            at = z * padded
            if low > start:
                blocks[j, at : at + low - start, :] = jnp.zeros((low - start, cols), F32)
            if high < start + padded:
                blocks[j, at + high - start : at + padded, :] = jnp.zeros(
                    (start + padded - high, cols), F32
                )
            blocks[j, at + low - start : at + high - start, :] = img[z, low:high, :]
    for z in range(depth):
        first = jnp.transpose(img[z, :, :LANE])
        last = jnp.transpose(img[z, :, cols - LANE :])
        edges[0, z * HALF : (z + 1) * HALF, :] = last[LANE - HALF :, :]
        edges[1, z * HALF : (z + 1) * HALF, :] = first[:HALF, :]
    sides = lax.div(lane + lanes - 1, lanes) + lax.div(2 * lanes - 2 - lane, lanes)
    pl.semaphore_wait(barrier, stacks - 1 + stacks * sides)

    def main_copy(j, source):
        return pltpu.make_async_remote_copy(
            src_ref=blocks.at[j],
            dst_ref=out.at[pl.ds(pl.multiple_of(source * size, 8), size), LANE : LANE + cols],
            send_sem=send.at[j],
            recv_sem=recv.at[source],
            device_id=(j, lane),
            device_id_type=MESH,
        )

    def side_copy(side, j, source, target):
        return pltpu.make_async_remote_copy(
            src_ref=edges.at[side],
            dst_ref=halo.at[side, pl.ds(pl.multiple_of(source * wide, 8), wide), :],
            send_sem=side_send.at[side, j],
            recv_sem=side_recv.at[side, source],
            device_id=(j, target),
            device_id_type=MESH,
        )

    def start(d, carry):
        j = lax.rem(here + lax.rem(d + stacks // 2, stacks), stacks)

        @pl.when(j != here)
        def _():
            main_copy(j, here).start()

        @pl.when(lane < lanes - 1)
        def _():
            side_copy(0, j, here, lane + 1).start()

        @pl.when(lane > 0)
        def _():
            side_copy(1, j, here, lane - 1).start()

        return carry

    lax.fori_loop(0, stacks, start, 0)
    out[pl.ds(pl.multiple_of(here * size, 8), size), LANE : LANE + cols] = blocks[here]

    def finish(d, carry):
        j = lax.rem(here + d, stacks)

        @pl.when(d > 0)
        def _():
            main_copy(j, here).wait_send()
            main_copy(j, j).wait_recv()

        @pl.when(lane < lanes - 1)
        def _():
            side_copy(0, j, here, lane + 1).wait_send()
            side_copy(1, j, j, lane + 1).wait_recv()

        @pl.when(lane > 0)
        def _():
            side_copy(1, j, here, lane - 1).wait_send()
            side_copy(0, j, j, lane - 1).wait_recv()

        return carry

    lax.fori_loop(0, stacks, finish, 0)
    for side in range(2):
        turned[:8, :] = jnp.zeros((8, LANE), F32)
        turned[8 + height :, :] = jnp.zeros((8, LANE), F32)
        turned[8 : 8 + height, :] = jnp.transpose(halo[side])
        strip = turned[pl.ds(here * rows + 8 - HALF, padded), :]
        for z in range(stacks * depth):
            place = LANE - HALF if side == 0 else LANE + cols
            out[z * padded : (z + 1) * padded, place : place + HALF] = strip[
                :, z * HALF : (z + 1) * HALF
            ]


def gather_kernel(pay, out, send, recv):
    here = lax.axis_index("gz")
    lane = lax.axis_index("xy")
    lanes = lax.axis_size("xy")
    barrier = pltpu.get_barrier_semaphore()
    for d in range(1, lanes):
        pl.semaphore_signal(
            barrier, inc=1, device_id=(here, lax.rem(lane + d, lanes)), device_id_type=MESH
        )
    pl.semaphore_wait(barrier, lanes - 1)

    def copy(target, source):
        return pltpu.make_async_remote_copy(
            src_ref=pay,
            dst_ref=out.at[source],
            send_sem=send.at[target],
            recv_sem=recv.at[source],
            device_id=(here, target),
            device_id_type=MESH,
        )

    for d in range(1, lanes):
        copy(lax.rem(lane + d, lanes), lane).start()
    out[lane] = pay[...]
    for d in range(1, lanes):
        other = lax.rem(lane + d, lanes)
        copy(other, lane).wait_send()
        copy(other, other).wait_recv()


def feature_kernel(
    img, ids, wide, tall, deep, owner, pay_ref, means_ref,
    shift, planar, highs_f, lows_f, acc, square, *pairs,
):
    depth, rows, cols = ids.shape
    padded_rows = rows + TAPS - 1
    fragments = means_ref.shape[1]
    highs = fragments // LO
    chans = means_ref.shape[0]
    lanes = pay_ref.shape[0] - chans
    for b in range(TAPS):
        for x in range(0, cols, LANE):
            start = LANE - HALF + b + x
            shift[b, x // LANE] = img[:, start : start + LANE]
    for e in range(HALF):
        planar[e] = jnp.zeros(planar.shape[1:], F32)
        planar[depth + HALF + e] = jnp.zeros(planar.shape[1:], F32)
    acc[...] = jnp.zeros(acc.shape, F32)

    def divide(z, carry):
        for x in range(0, cols, LANE):
            part = ids[z, :, x : x + LANE]
            highs_f[x // LANE, z] = (part >> (LO.bit_length() - 1)).astype(F32)
            lows_f[x // LANE, z] = (part & (LO - 1)).astype(F32)
        return carry

    lax.fori_loop(0, depth, divide, 0)
    square[...] = jnp.zeros(square.shape, F32)
    for kind, part in enumerate((wide, tall, deep)):
        square[kind * 8 : kind * 8 + TAPS, :chans] = part[...]
    turned = jnp.transpose(square[...])
    tap = [
        jnp.broadcast_to(turned[:chans, k * 8 + i : k * 8 + i + 1], (chans, LANE))
        for k in range(3)
        for i in range(TAPS)
    ]

    def plane(z, carry):
        for x in range(0, cols, LANE):
            window = []
            for y in range(padded_rows):
                total = None
                for b in range(TAPS):
                    row = shift[b, x // LANE, pl.ds(z * padded_rows + y, 1), :]
                    term = tap[b] * jnp.broadcast_to(row, (chans, LANE))
                    total = term if total is None else total + term
                window.append(total)
                if y >= TAPS - 1:
                    total = tap[TAPS] * window[y - TAPS + 1]
                    for a in range(1, TAPS):
                        total = total + tap[TAPS + a] * window[y - TAPS + 1 + a]
                    planar[z + HALF, y - TAPS + 1, :, x : x + LANE] = total.astype(BF16).astype(F32)
        return carry

    lax.fori_loop(0, depth, plane, 0)
    low_line = lax.broadcasted_iota(jnp.int32, (LO, LANE), 0).astype(F32).astype(BF16)
    one = jnp.ones((16, LANE), BF16)
    zero = jnp.zeros((16, LANE), BF16)

    per_plane = rows // ROWS
    steps = depth * per_plane

    def build(step, left, right):
        z = step // per_plane
        base = (step % per_plane) * ROWS
        for r in range(ROWS):
            y = base + r
            for x in range(0, cols, LANE):
                at = r * cols + x
                total = tap[2 * TAPS] * planar[z, y, :, x : x + LANE]
                for e in range(1, TAPS):
                    total = total + tap[2 * TAPS + e] * planar[z + e, y, :, x : x + LANE]
                feat = jnp.tanh(total).astype(BF16)
                high = highs_f[x // LANE, z, pl.ds(y, 1), :]
                high = jnp.broadcast_to(high, (16, LANE)).astype(BF16)
                low = lows_f[x // LANE, z, pl.ds(y, 1), :]
                low = jnp.broadcast_to(low, (16, LANE)).astype(BF16)
                for h in range(highs):
                    left[h * 16 : (h + 1) * 16, at : at + LANE] = jnp.where(
                        high == jnp.full((16, LANE), h, BF16), feat, zero
                    )
                left[highs * 16 :, at : at + LANE] = jnp.where(high == low_line[:16], one, zero)
                for k in range(LO // 16):
                    right[k * 16 : (k + 1) * 16, at : at + LANE] = jnp.where(
                        low == low_line[k * 16 : (k + 1) * 16], one, zero
                    )

    def fire(left, right):
        acc[...] += lax.dot_general(
            left[...], right[...], (((1,), (1,)), ((), ())), preferred_element_type=F32
        )

    left_a, right_a, left_b, right_b = pairs
    build(0, left_a, right_a)

    def two_steps(pair, carry):
        fire(left_a, right_a)
        build(2 * pair + 1, left_b, right_b)
        fire(left_b, right_b)
        build(jnp.minimum(2 * pair + 2, steps - 1), left_a, right_a)
        return carry

    lax.fori_loop(0, steps // 2, two_steps, 0)
    for h in range(highs):
        count = acc[highs * chans + h : highs * chans + h + 1, :]
        mean = acc[h * chans : (h + 1) * chans, :] / count
        means_ref[:, h * LO : (h + 1) * LO] = mean
        pay_ref[:chans, h * LO : (h + 1) * LO] = mean
        own = jnp.broadcast_to(owner[:, h * LO : (h + 1) * LO], (lanes, LO))
        line = lax.broadcasted_iota(jnp.int32, (lanes, LO), 0)
        pay_ref[chans:, h * LO : (h + 1) * LO] = jnp.where(
            own == line, jnp.broadcast_to(count, (lanes, LO)), 0.0
        )


def split3(x):
    high = x.astype(BF16)
    rest = x - high.astype(F32)
    mid = rest.astype(BF16)
    low = (rest - mid.astype(F32)).astype(BF16)
    return high, mid, low


def refine_kernel(pseudo, pay, coarse, parent, offsets, out_ref, factors, norms):
    sources, _, fragments = pay.shape
    chans = out_ref.shape[0]
    own = chans + lax.axis_index("xy")
    coarse_count = coarse.shape[1]
    fine = out_ref.shape[1]
    select = (
        jnp.broadcast_to(parent[...], (coarse_count, fine))
        == lax.broadcasted_iota(jnp.int32, (coarse_count, fine), 0)
    ).astype(F32)
    cents = jnp.dot(coarse[...], select, precision=HIGH, preferred_element_type=F32) + offsets[...]

    def prepare(s, carry):
        frags = pay[s, :chans, :]
        fh, fm, fl = split3(-2.0 * frags)
        ones = jnp.ones((3 * chans, fragments), BF16)
        factors[s] = jnp.concatenate([fh, fm, fh, fl, fm, fh, ones], axis=0)
        norms[s] = jnp.sum(frags * frags, axis=0, keepdims=True)
        return carry

    lax.fori_loop(0, sources, prepare, 0, unroll=4)
    for step in range(ITERS):
        ch, cm, cl = split3(cents)
        sh, sm, sl = split3(cents * cents)
        keys = jnp.concatenate([ch, ch, cm, ch, cm, cl, sh, sm, sl], axis=0)

        def visit(s, total):
            distance = norms[s] + lax.dot_general(
                keys, factors[s], (((0,), (0,)), ((), ())), preferred_element_type=F32
            )
            scores = -sharpness * distance
            top = jnp.max(scores, axis=0, keepdims=True)
            expo = jnp.exp(scores - top)
            scale = pay[s, pl.ds(own, 1), :] / jnp.sum(expo, axis=0, keepdims=True)
            scale = jnp.broadcast_to(scale, (chans, fragments))
            gh, gm, gl = split3(jnp.concatenate([pay[s, :chans, :] * scale, scale], axis=0))
            eh, em, el = split3(expo)
            dims = (((1,), (1,)), ((), ()))
            first = lax.dot_general(
                jnp.concatenate([gh, gm, gl], axis=0), eh, dims, preferred_element_type=F32
            )
            second = lax.dot_general(
                jnp.concatenate([gh, gm], axis=0), em, dims, preferred_element_type=F32
            )
            size = 2 * chans
            return (
                total
                + (first[2 * size :] + second[size:])
                + (first[size : 2 * size] + second[:size])
                + first[:size]
            )

        total = lax.fori_loop(
            0, sources, visit, jnp.zeros((2 * chans, fine), F32), unroll=4
        )
        cents = (total[:chans] + pseudo * cents) / (total[chans:] + pseudo)
    out_ref[...] = cents


def shards(
    slab_image,
    width_taps,
    height_taps,
    depth_taps,
    fragment_ids,
    fragment_owner,
    coarse_centroids,
    parent_map,
    fine_offsets,
):
    chans = width_taps.shape[0]
    depth, rows, cols = fragment_ids.shape
    fragments = fragment_owner.shape[0]
    lanes = lax.axis_size("xy")
    stacks = lax.axis_size("gz")
    padded_rows = rows + TAPS - 1
    slab_depth, height, _ = slab_image.shape
    pencil = pl.pallas_call(
        functools.partial(exchange_kernel, rows),
        out_shape=jax.ShapeDtypeStruct((depth * padded_rows, cols + 2 * LANE), F32),
        in_specs=[pl.BlockSpec(memory_space=pltpu.VMEM)],
        out_specs=pl.BlockSpec(memory_space=pltpu.VMEM),
        scratch_shapes=[
            pltpu.VMEM((stacks, slab_depth * padded_rows, cols), F32),
            pltpu.VMEM((2, slab_depth * HALF, height), F32),
            pltpu.VMEM((2, LANE, height), F32),
            pltpu.VMEM((height + 16, LANE), F32),
            pltpu.SemaphoreType.DMA((stacks,)),
            pltpu.SemaphoreType.DMA((stacks,)),
            pltpu.SemaphoreType.DMA((2, stacks)),
            pltpu.SemaphoreType.DMA((2, stacks)),
        ],
        compiler_params=pltpu.CompilerParams(
            collective_id=0, has_side_effects=True, vmem_limit_bytes=32 << 20
        ),
        name="exchange",
    )(slab_image)
    highs = fragments // LO
    assert highs <= 16
    pay, means = pl.pallas_call(
        feature_kernel,
        out_shape=(
            jax.ShapeDtypeStruct((chans + lanes, fragments), F32),
            jax.ShapeDtypeStruct((chans, fragments), F32),
        ),
        in_specs=[pl.BlockSpec(memory_space=pltpu.VMEM)] * 6,
        out_specs=(pl.BlockSpec(memory_space=pltpu.VMEM),) * 2,
        scratch_shapes=[
            pltpu.VMEM((TAPS, cols // LANE, depth * padded_rows, LANE), F32),
            pltpu.VMEM((depth + 2 * HALF, rows, chans, cols), F32),
            pltpu.VMEM((cols // LANE, depth, rows, LANE), F32),
            pltpu.VMEM((cols // LANE, depth, rows, LANE), F32),
            pltpu.VMEM((highs * chans + 16, LO), F32),
            pltpu.VMEM((LANE, LANE), F32),
            pltpu.VMEM((highs * chans + 16, ROWS * cols), BF16),
            pltpu.VMEM((LO, ROWS * cols), BF16),
            pltpu.VMEM((highs * chans + 16, ROWS * cols), BF16),
            pltpu.VMEM((LO, ROWS * cols), BF16),
        ],
        compiler_params=pltpu.CompilerParams(vmem_limit_bytes=56 << 20),
        name="features",
    )(pencil, fragment_ids, width_taps.T, height_taps.T, depth_taps.T, fragment_owner.reshape(1, fragments))
    gathered = pl.pallas_call(
        gather_kernel,
        out_shape=jax.ShapeDtypeStruct((lanes,) + pay.shape, F32),
        in_specs=[pl.BlockSpec(memory_space=pltpu.VMEM)],
        out_specs=pl.BlockSpec(memory_space=pltpu.VMEM),
        scratch_shapes=[pltpu.SemaphoreType.DMA((lanes,)), pltpu.SemaphoreType.DMA((lanes,))],
        compiler_params=pltpu.CompilerParams(
            collective_id=1, has_side_effects=True, vmem_limit_bytes=32 << 20
        ),
        name="gather",
    )(pay)
    fine = fine_offsets.shape[1]
    pseudo = float(fragment_ids.size // fine)
    centroids = pl.pallas_call(
        functools.partial(refine_kernel, pseudo),
        out_shape=jax.ShapeDtypeStruct((chans, fine), F32),
        in_specs=[pl.BlockSpec(memory_space=pltpu.VMEM)] * 4,
        out_specs=pl.BlockSpec(memory_space=pltpu.VMEM),
        scratch_shapes=[
            pltpu.VMEM((lanes, 9 * chans, fragments), BF16),
            pltpu.VMEM((lanes, 1, fragments), F32),
        ],
        compiler_params=pltpu.CompilerParams(vmem_limit_bytes=48 << 20),
        name="refine",
    )(gathered, coarse_centroids, parent_map.reshape(1, fine), fine_offsets)
    return (means, centroids)


def solution(mesh):
    placed = (
        P("gz", None, "xy"),
        P(),
        P(),
        P(),
        P(None, "gz", "xy"),
        P(("gz", "xy"), None),
        P(None, ("gz", "xy")),
        P(("gz", "xy")),
        P(None, ("gz", "xy")),
    )
    return jax.shard_map(
        shards,
        mesh=mesh,
        in_specs=placed,
        out_specs=(P(None, ("gz", "xy")), P(None, ("gz", "xy"))),
        check_vma=False,
    )
```

```python
import functools

import jax
import jax.numpy as jnp
from jax import lax
from jax.experimental import pallas as pl
from jax.experimental.pallas import tpu as pltpu
from jax.sharding import PartitionSpec as P

TAPS = 5
HALF = TAPS // 2
ITERS = 3
HIGH = lax.Precision.HIGHEST
sharpness = 2.0
LO = 128
ROWS = 16
F32 = jnp.float32
BF16 = jnp.bfloat16


MESH = pl.DeviceIdType.MESH
LANE = 128


def exchange_kernel(rows, img, out, blocks, edges, halo, turned, send, recv, side_send, side_recv):
    here = lax.axis_index("gz")
    lane = lax.axis_index("xy")
    stacks = lax.axis_size("gz")
    lanes = lax.axis_size("xy")
    depth, height, cols = img.shape
    padded = rows + TAPS - 1
    size = depth * padded
    wide = depth * HALF

    for side in range(2):
        if stacks * wide < LANE:
            halo[side, stacks * wide :, :] = jnp.zeros((LANE - stacks * wide, height), F32)

    @pl.when(lane == 0)
    def _():
        halo[0] = jnp.zeros(halo.shape[1:], F32)

    @pl.when(lane == lanes - 1)
    def _():
        halo[1] = jnp.zeros(halo.shape[1:], F32)

    barrier = pltpu.get_barrier_semaphore()

    def greet(d, carry):
        j = lax.rem(here + d, stacks)

        @pl.when(d > 0)
        def _():
            pl.semaphore_signal(barrier, inc=1, device_id=(j, lane), device_id_type=MESH)

        @pl.when(lane > 0)
        def _():
            pl.semaphore_signal(barrier, inc=1, device_id=(j, lane - 1), device_id_type=MESH)

        @pl.when(lane < lanes - 1)
        def _():
            pl.semaphore_signal(barrier, inc=1, device_id=(j, lane + 1), device_id_type=MESH)

        return carry

    lax.fori_loop(0, stacks, greet, 0)
    for j in range(stacks):
        for z in range(depth):
            start = j * rows - HALF
            low, high = max(start, 0), min(start + padded, height)
            at = z * padded
            if low > start:
                blocks[j, at : at + low - start, :] = jnp.zeros((low - start, cols), F32)
            if high < start + padded:
                blocks[j, at + high - start : at + padded, :] = jnp.zeros(
                    (start + padded - high, cols), F32
                )
            blocks[j, at + low - start : at + high - start, :] = img[z, low:high, :]
    for z in range(depth):
        first = jnp.transpose(img[z, :, :LANE])
        last = jnp.transpose(img[z, :, cols - LANE :])
        edges[0, z * HALF : (z + 1) * HALF, :] = last[LANE - HALF :, :]
        edges[1, z * HALF : (z + 1) * HALF, :] = first[:HALF, :]
    sides = lax.div(lane + lanes - 1, lanes) + lax.div(2 * lanes - 2 - lane, lanes)
    pl.semaphore_wait(barrier, stacks - 1 + stacks * sides)

    def main_copy(j, source):
        return pltpu.make_async_remote_copy(
            src_ref=blocks.at[j],
            dst_ref=out.at[pl.ds(pl.multiple_of(source * size, 8), size), LANE : LANE + cols],
            send_sem=send.at[j],
            recv_sem=recv.at[source],
            device_id=(j, lane),
            device_id_type=MESH,
        )

    def side_copy(side, j, source, target):
        return pltpu.make_async_remote_copy(
            src_ref=edges.at[side],
            dst_ref=halo.at[side, pl.ds(pl.multiple_of(source * wide, 8), wide), :],
            send_sem=side_send.at[side, j],
            recv_sem=side_recv.at[side, source],
            device_id=(j, target),
            device_id_type=MESH,
        )

    def start(d, carry):
        j = lax.rem(here + d, stacks)

        @pl.when(d > 0)
        def _():
            main_copy(j, here).start()

        @pl.when(lane < lanes - 1)
        def _():
            side_copy(0, j, here, lane + 1).start()

        @pl.when(lane > 0)
        def _():
            side_copy(1, j, here, lane - 1).start()

        return carry

    lax.fori_loop(0, stacks, start, 0)
    out[pl.ds(pl.multiple_of(here * size, 8), size), LANE : LANE + cols] = blocks[here]

    def finish(d, carry):
        j = lax.rem(here + d, stacks)

        @pl.when(d > 0)
        def _():
            main_copy(j, here).wait_send()
            main_copy(j, j).wait_recv()

        @pl.when(lane < lanes - 1)
        def _():
            side_copy(0, j, here, lane + 1).wait_send()
            side_copy(1, j, j, lane + 1).wait_recv()

        @pl.when(lane > 0)
        def _():
            side_copy(1, j, here, lane - 1).wait_send()
            side_copy(0, j, j, lane - 1).wait_recv()

        return carry

    lax.fori_loop(0, stacks, finish, 0)
    for side in range(2):
        turned[:8, :] = jnp.zeros((8, LANE), F32)
        turned[8 + height :, :] = jnp.zeros((8, LANE), F32)
        turned[8 : 8 + height, :] = jnp.transpose(halo[side])
        strip = turned[pl.ds(here * rows + 8 - HALF, padded), :]
        for z in range(stacks * depth):
            place = LANE - HALF if side == 0 else LANE + cols
            out[z * padded : (z + 1) * padded, place : place + HALF] = strip[
                :, z * HALF : (z + 1) * HALF
            ]


def gather_kernel(pay, out, send, recv):
    here = lax.axis_index("gz")
    lane = lax.axis_index("xy")
    lanes = lax.axis_size("xy")
    barrier = pltpu.get_barrier_semaphore()
    for d in range(1, lanes):
        pl.semaphore_signal(
            barrier, inc=1, device_id=(here, lax.rem(lane + d, lanes)), device_id_type=MESH
        )
    pl.semaphore_wait(barrier, lanes - 1)

    def copy(target, source):
        return pltpu.make_async_remote_copy(
            src_ref=pay,
            dst_ref=out.at[source],
            send_sem=send.at[target],
            recv_sem=recv.at[source],
            device_id=(here, target),
            device_id_type=MESH,
        )

    for d in range(1, lanes):
        copy(lax.rem(lane + d, lanes), lane).start()
    out[lane] = pay[...]
    for d in range(1, lanes):
        other = lax.rem(lane + d, lanes)
        copy(other, lane).wait_send()
        copy(other, other).wait_recv()


def feature_kernel(
    img, ids, wide, tall, deep, owner, pay_ref, means_ref,
    shift, planar, highs_f, lows_f, acc, square, *pairs,
):
    depth, rows, cols = ids.shape
    padded_rows = rows + TAPS - 1
    fragments = means_ref.shape[1]
    highs = fragments // LO
    chans = means_ref.shape[0]
    lanes = pay_ref.shape[0] - chans
    for b in range(TAPS):
        for x in range(0, cols, LANE):
            start = LANE - HALF + b + x
            shift[b, x // LANE] = img[:, start : start + LANE]
    for e in range(HALF):
        planar[e] = jnp.zeros(planar.shape[1:], F32)
        planar[depth + HALF + e] = jnp.zeros(planar.shape[1:], F32)
    acc[...] = jnp.zeros(acc.shape, F32)

    def divide(z, carry):
        for x in range(0, cols, LANE):
            part = ids[z, :, x : x + LANE]
            highs_f[x // LANE, z] = (part >> (LO.bit_length() - 1)).astype(F32)
            lows_f[x // LANE, z] = (part & (LO - 1)).astype(F32)
        return carry

    lax.fori_loop(0, depth, divide, 0)
    square[...] = jnp.zeros(square.shape, F32)
    for kind, part in enumerate((wide, tall, deep)):
        square[kind * 8 : kind * 8 + TAPS, :chans] = part[...]
    turned = jnp.transpose(square[...])
    tap = [
        jnp.broadcast_to(turned[:chans, k * 8 + i : k * 8 + i + 1], (chans, LANE))
        for k in range(3)
        for i in range(TAPS)
    ]

    def plane(z, carry):
        for x in range(0, cols, LANE):
            window = []
            for y in range(padded_rows):
                total = None
                for b in range(TAPS):
                    row = shift[b, x // LANE, pl.ds(z * padded_rows + y, 1), :]
                    term = tap[b] * jnp.broadcast_to(row, (chans, LANE))
                    total = term if total is None else total + term
                window.append(total)
                if y >= TAPS - 1:
                    total = tap[TAPS] * window[y - TAPS + 1]
                    for a in range(1, TAPS):
                        total = total + tap[TAPS + a] * window[y - TAPS + 1 + a]
                    planar[z + HALF, y - TAPS + 1, :, x : x + LANE] = total.astype(BF16).astype(F32)
        return carry

    lax.fori_loop(0, depth, plane, 0)
    low_line = lax.broadcasted_iota(jnp.int32, (LO, LANE), 0).astype(F32).astype(BF16)
    one = jnp.ones((16, LANE), BF16)
    zero = jnp.zeros((16, LANE), BF16)

    per_plane = rows // ROWS
    steps = depth * per_plane

    def build(step, left, right):
        z = step // per_plane
        base = (step % per_plane) * ROWS
        for r in range(ROWS):
            y = base + r
            for x in range(0, cols, LANE):
                at = r * cols + x
                total = tap[2 * TAPS] * planar[z, y, :, x : x + LANE]
                for e in range(1, TAPS):
                    total = total + tap[2 * TAPS + e] * planar[z + e, y, :, x : x + LANE]
                feat = jnp.tanh(total).astype(BF16)
                high = highs_f[x // LANE, z, pl.ds(y, 1), :]
                high = jnp.broadcast_to(high, (16, LANE)).astype(BF16)
                low = lows_f[x // LANE, z, pl.ds(y, 1), :]
                low = jnp.broadcast_to(low, (16, LANE)).astype(BF16)
                for h in range(highs):
                    left[h * 16 : (h + 1) * 16, at : at + LANE] = jnp.where(
                        high == jnp.full((16, LANE), h, BF16), feat, zero
                    )
                left[highs * 16 :, at : at + LANE] = jnp.where(high == low_line[:16], one, zero)
                for k in range(LO // 16):
                    right[k * 16 : (k + 1) * 16, at : at + LANE] = jnp.where(
                        low == low_line[k * 16 : (k + 1) * 16], one, zero
                    )

    def fire(left, right):
        acc[...] += lax.dot_general(
            left[...], right[...], (((1,), (1,)), ((), ())), preferred_element_type=F32
        )

    left_a, right_a, left_b, right_b = pairs
    build(0, left_a, right_a)

    def two_steps(pair, carry):
        fire(left_a, right_a)
        build(2 * pair + 1, left_b, right_b)
        fire(left_b, right_b)
        build(jnp.minimum(2 * pair + 2, steps - 1), left_a, right_a)
        return carry

    lax.fori_loop(0, steps // 2, two_steps, 0)
    for h in range(highs):
        count = acc[highs * chans + h : highs * chans + h + 1, :]
        mean = acc[h * chans : (h + 1) * chans, :] / count
        means_ref[:, h * LO : (h + 1) * LO] = mean
        pay_ref[:chans, h * LO : (h + 1) * LO] = mean
        own = jnp.broadcast_to(owner[:, h * LO : (h + 1) * LO], (lanes, LO))
        line = lax.broadcasted_iota(jnp.int32, (lanes, LO), 0)
        pay_ref[chans:, h * LO : (h + 1) * LO] = jnp.where(
            own == line, jnp.broadcast_to(count, (lanes, LO)), 0.0
        )


def split3(x):
    high = x.astype(BF16)
    rest = x - high.astype(F32)
    mid = rest.astype(BF16)
    low = (rest - mid.astype(F32)).astype(BF16)
    return high, mid, low


def refine_kernel(pseudo, pay, coarse, parent, offsets, out_ref, factors, norms):
    sources, _, fragments = pay.shape
    chans = out_ref.shape[0]
    own = chans + lax.axis_index("xy")
    coarse_count = coarse.shape[1]
    fine = out_ref.shape[1]
    select = (
        jnp.broadcast_to(parent[...], (coarse_count, fine))
        == lax.broadcasted_iota(jnp.int32, (coarse_count, fine), 0)
    ).astype(F32)
    cents = jnp.dot(coarse[...], select, precision=HIGH, preferred_element_type=F32) + offsets[...]

    def prepare(s, carry):
        frags = pay[s, :chans, :]
        fh, fm, fl = split3(-2.0 * frags)
        ones = jnp.ones((3 * chans, fragments), BF16)
        factors[s] = jnp.concatenate([fh, fm, fh, fl, fm, fh, ones], axis=0)
        norms[s] = jnp.sum(frags * frags, axis=0, keepdims=True)
        return carry

    lax.fori_loop(0, sources, prepare, 0, unroll=4)
    for step in range(ITERS):
        ch, cm, cl = split3(cents)
        sh, sm, sl = split3(cents * cents)
        keys = jnp.concatenate([ch, ch, cm, ch, cm, cl, sh, sm, sl], axis=0)

        def visit(s, total):
            distance = norms[s] + lax.dot_general(
                keys, factors[s], (((0,), (0,)), ((), ())), preferred_element_type=F32
            )
            scores = -sharpness * distance
            top = jnp.max(scores, axis=0, keepdims=True)
            expo = jnp.exp(scores - top)
            scale = pay[s, pl.ds(own, 1), :] / jnp.sum(expo, axis=0, keepdims=True)
            scale = jnp.broadcast_to(scale, (chans, fragments))
            gh, gm, gl = split3(jnp.concatenate([pay[s, :chans, :] * scale, scale], axis=0))
            eh, em, el = split3(expo)
            dims = (((1,), (1,)), ((), ()))
            first = lax.dot_general(
                jnp.concatenate([gh, gm, gl], axis=0), eh, dims, preferred_element_type=F32
            )
            second = lax.dot_general(
                jnp.concatenate([gh, gm], axis=0), em, dims, preferred_element_type=F32
            )
            size = 2 * chans
            return (
                total
                + (first[2 * size :] + second[size:])
                + (first[size : 2 * size] + second[:size])
                + first[:size]
            )

        total = lax.fori_loop(
            0, sources, visit, jnp.zeros((2 * chans, fine), F32), unroll=4
        )
        cents = (total[:chans] + pseudo * cents) / (total[chans:] + pseudo)
    out_ref[...] = cents


def shards(
    slab_image,
    width_taps,
    height_taps,
    depth_taps,
    fragment_ids,
    fragment_owner,
    coarse_centroids,
    parent_map,
    fine_offsets,
):
    chans = width_taps.shape[0]
    depth, rows, cols = fragment_ids.shape
    fragments = fragment_owner.shape[0]
    lanes = lax.axis_size("xy")
    stacks = lax.axis_size("gz")
    padded_rows = rows + TAPS - 1
    slab_depth, height, _ = slab_image.shape
    pencil = pl.pallas_call(
        functools.partial(exchange_kernel, rows),
        out_shape=jax.ShapeDtypeStruct((depth * padded_rows, cols + 2 * LANE), F32),
        in_specs=[pl.BlockSpec(memory_space=pltpu.VMEM)],
        out_specs=pl.BlockSpec(memory_space=pltpu.VMEM),
        scratch_shapes=[
            pltpu.VMEM((stacks, slab_depth * padded_rows, cols), F32),
            pltpu.VMEM((2, slab_depth * HALF, height), F32),
            pltpu.VMEM((2, LANE, height), F32),
            pltpu.VMEM((height + 16, LANE), F32),
            pltpu.SemaphoreType.DMA((stacks,)),
            pltpu.SemaphoreType.DMA((stacks,)),
            pltpu.SemaphoreType.DMA((2, stacks)),
            pltpu.SemaphoreType.DMA((2, stacks)),
        ],
        compiler_params=pltpu.CompilerParams(
            collective_id=0, has_side_effects=True, vmem_limit_bytes=32 << 20
        ),
        name="exchange",
    )(slab_image)
    highs = fragments // LO
    assert highs <= 16
    grant = (16 << 20) + 144 * depth * rows * cols
    pay, means = pl.pallas_call(
        feature_kernel,
        out_shape=(
            jax.ShapeDtypeStruct((chans + lanes, fragments), F32),
            jax.ShapeDtypeStruct((chans, fragments), F32),
        ),
        in_specs=[pl.BlockSpec(memory_space=pltpu.VMEM)] * 6,
        out_specs=(pl.BlockSpec(memory_space=pltpu.VMEM),) * 2,
        scratch_shapes=[
            pltpu.VMEM((TAPS, cols // LANE, depth * padded_rows, LANE), F32),
            pltpu.VMEM((depth + 2 * HALF, rows, chans, cols), F32),
            pltpu.VMEM((cols // LANE, depth, rows, LANE), F32),
            pltpu.VMEM((cols // LANE, depth, rows, LANE), F32),
            pltpu.VMEM((highs * chans + 16, LO), F32),
            pltpu.VMEM((LANE, LANE), F32),
            pltpu.VMEM((highs * chans + 16, ROWS * cols), BF16),
            pltpu.VMEM((LO, ROWS * cols), BF16),
            pltpu.VMEM((highs * chans + 16, ROWS * cols), BF16),
            pltpu.VMEM((LO, ROWS * cols), BF16),
        ],
        compiler_params=pltpu.CompilerParams(vmem_limit_bytes=grant),
        name="features",
    )(pencil, fragment_ids, width_taps.T, height_taps.T, depth_taps.T, fragment_owner.reshape(1, fragments))
    gathered = pl.pallas_call(
        gather_kernel,
        out_shape=jax.ShapeDtypeStruct((lanes,) + pay.shape, F32),
        in_specs=[pl.BlockSpec(memory_space=pltpu.VMEM)],
        out_specs=pl.BlockSpec(memory_space=pltpu.VMEM),
        scratch_shapes=[pltpu.SemaphoreType.DMA((lanes,)), pltpu.SemaphoreType.DMA((lanes,))],
        compiler_params=pltpu.CompilerParams(
            collective_id=1, has_side_effects=True, vmem_limit_bytes=16 << 20
        ),
        name="gather",
    )(pay)
    fine = fine_offsets.shape[1]
    pseudo = float(fragment_ids.size // fine)
    centroids = pl.pallas_call(
        functools.partial(refine_kernel, pseudo),
        out_shape=jax.ShapeDtypeStruct((chans, fine), F32),
        in_specs=[pl.BlockSpec(memory_space=pltpu.VMEM)] * 4,
        out_specs=pl.BlockSpec(memory_space=pltpu.VMEM),
        scratch_shapes=[
            pltpu.VMEM((lanes, 9 * chans, fragments), BF16),
            pltpu.VMEM((lanes, 1, fragments), F32),
        ],
        compiler_params=pltpu.CompilerParams(vmem_limit_bytes=48 << 20),
        name="refine",
    )(gathered, coarse_centroids, parent_map.reshape(1, fine), fine_offsets)
    return (means, centroids)


def solution(mesh):
    placed = (
        P("gz", None, "xy"),
        P(),
        P(),
        P(),
        P(None, "gz", "xy"),
        P(("gz", "xy"), None),
        P(None, ("gz", "xy")),
        P(("gz", "xy")),
        P(None, ("gz", "xy")),
    )
    return jax.shard_map(
        shards,
        mesh=mesh,
        in_specs=placed,
        out_specs=(P(None, ("gz", "xy")), P(None, ("gz", "xy"))),
        check_vma=False,
    )
```
